32 devices in a mesh: group: 4 (over x, core), head: 8 (over z, y).
Axes of the slice: x: 2, y: 2, z: 4, core: 2. Of those that a mesh axis runs over, the one named last changes fastest.
Arguments:
- qkv: bfloat16 [2048, 3, 512], P(('group', 'head')), may hold values from -40 to 40
- pattern: int32 [4, 3, 8, 6], P('group'), may hold values from 0 to 7, as said below
- counts: int32 [4, 3, 8], P('group'), may hold values from 0 to 6, as said below
Outputs:
- attended: bfloat16 [2048, 512], P(('group', 'head'))
The draws below stay inside these ranges and needn't reach their ends.
Inputs may be any that keep to these rules, and one draw needn't show every extreme that they name: `pattern`: within one list (g, j, n) the 6 blocks are distinct; at offset index 1 the first entry of query block n's list is n. `counts`: at offset index 1 every count is 1 or more; some count equals 6.
All inputs are finite; a program needn't handle non-finite values.
Results may differ from the reference program's by a relative error of at most 0.0044.
Values may be sent and summed in bfloat16 or wider, within the bound.
No kernel may reach another device: no remote copies, remote signals or barrier semaphores. Data moves between devices by JAX's collectives and lax.ppermute only.
A program may use at most 64 MiB of HBM per device.

```python
import jax
import jax.numpy as jnp
from jax import lax

TOK_DEV = 64
HEAD_DIM = 64
BLOCK = 64
KS = 6
HEADS = 8
INNER = 512
NB = 8
HALF = 1
CYCLE = 3
TOKENS = 2048
N_GROUP = 4
N_HEAD = 8


def draw_qkv(key, part):
    whole = jnp.clip(1.6 * jax.random.normal(key, (TOKENS, 3, INNER), jnp.float32), -9.6, 9.6)
    return whole.astype(jnp.bfloat16)


def draw_pattern(key, part):
    scores = jax.random.randint(key, (N_GROUP, CYCLE, NB, NB), 0, 65536)
    ident = jnp.arange(NB, dtype=jnp.int32)
    distinct = scores * NB + ident[None, None, None, :]
    own = (jnp.arange(CYCLE, dtype=jnp.int32) == HALF)[None, :, None, None] & (ident[:, None] == ident[None, :])[None, None, :, :]
    distinct = jnp.where(own, -1, distinct)
    order = jnp.argsort(distinct, axis=-1, stable=True)
    return order[..., :KS].astype(jnp.int32)


def draw_counts(key, part):
    key_level = jax.random.fold_in(key, 11)
    key_count = jax.random.fold_in(key, 12)
    level = jax.random.randint(key_level, (N_GROUP, 1, 1), 1, KS + 1)
    raw = jax.random.randint(key_count, (N_GROUP, CYCLE, NB), 0, KS + 1)
    counts = jnp.minimum(raw, level)
    own = (jnp.arange(CYCLE, dtype=jnp.int32) == HALF)[None, :, None]
    counts = jnp.where(own, jnp.maximum(counts, 1), counts)
    counts = counts.at[0, HALF, 0].set(KS)
    return counts.astype(jnp.int32)


def setup_inputs(seed: int = 0) -> dict:
    streams_of = jax.random.split(jax.random.key(seed), 4)
    return {
        "qkv": draw_qkv(jax.random.fold_in(streams_of[3], 71), 0),
        "pattern": draw_pattern(jax.random.fold_in(streams_of[3], 71), 0),
        "counts": draw_counts(jax.random.fold_in(streams_of[3], 71), 0),
    }


def reference(qkv, pattern, counts):
    group_rows = TOK_DEV * N_HEAD
    blocks = group_rows // BLOCK
    data = qkv.reshape(N_GROUP, group_rows, 3, HEADS, HEAD_DIM)
    per_head = jnp.moveaxis(data, 3, 0)
    scale = HEAD_DIM ** -0.5

    def one_head(head_data):
        def one_group(group_index):
            query = head_data[group_index, :, 0].reshape(blocks, BLOCK, HEAD_DIM).astype(jnp.float32)
            keys_all = []
            values_all = []
            live_all = []
            for offset in range(CYCLE):
                source_index = (group_index + offset - HALF) % N_GROUP
                source = lax.dynamic_index_in_dim(head_data, source_index, 0, keepdims=False)
                tiles = source[:, 1:].reshape(blocks, BLOCK, 2, HEAD_DIM)[pattern[group_index, offset]]
                keys_all.append(tiles[:, :, :, 0, :].reshape(blocks, KS * BLOCK, HEAD_DIM))
                values_all.append(tiles[:, :, :, 1, :].reshape(blocks, KS * BLOCK, HEAD_DIM))
                entry_live = jnp.arange(KS, dtype=jnp.int32)[None, :] < counts[group_index, offset][:, None]
                live_all.append(jnp.repeat(entry_live, BLOCK, axis=1))
            keys = jnp.concatenate(keys_all, axis=1).astype(jnp.float32)
            values = jnp.concatenate(values_all, axis=1).astype(jnp.float32)
            live = jnp.concatenate(live_all, axis=1)
            scores = jnp.einsum('nqd,nkd->nqk', query, keys) * scale
            scores = jnp.where(live[:, None, :], scores, -jnp.inf)
            top = scores.max(axis=-1, keepdims=True)
            weights = jnp.exp(scores - top)
            total = weights.sum(axis=-1, keepdims=True)
            rounded = weights.astype(jnp.bfloat16).astype(jnp.float32)
            output = jnp.einsum('nqk,nkd->nqd', rounded, values) / total
            return output.astype(jnp.bfloat16).reshape(group_rows, HEAD_DIM)

        return lax.map(one_group, jnp.arange(N_GROUP, dtype=jnp.int32))

    result = lax.map(one_head, per_head)
    return jnp.transpose(result, (1, 2, 0, 3)).reshape(TOKENS, HEADS * HEAD_DIM)
```

```python
import functools
import math

import jax
import jax.numpy as jnp
from jax import lax
from jax.experimental import pallas as pl
from jax.experimental.pallas import tpu as pltpu
from jax.sharding import PartitionSpec as P

LOG2E = 1.4426950408889634
VMEM = pltpu.MemorySpace.VMEM
SMEM = pltpu.MemorySpace.SMEM


def lanes_of(shape):
    return lax.broadcasted_iota(jnp.int32, shape, len(shape) - 1)


def rows_dot(left, right):
    return lax.dot_general(
        left, right, (((1,), (1,)), ((), ())), preferred_element_type=jnp.float32
    )


def pack_kernel(dim, x_ref, o_ref):
    tokens = x_ref.shape[1]
    half = tokens // 2
    for head in range(o_ref.shape[0]):
        cols = slice(head * dim, (head + 1) * dim)
        o_ref[head, :tokens] = jnp.concatenate([x_ref[1, :, cols], x_ref[2, :, cols]], axis=-1)
        o_ref[head, tokens:] = jnp.concatenate(
            [x_ref[0, :half, cols], x_ref[0, half:, cols]], axis=-1
        )


def unpack_kernel(dim, x_ref, o_ref):
    half = x_ref.shape[1]
    for pair in range(x_ref.shape[0] // 2):
        one, two = x_ref[2 * pair], x_ref[2 * pair + 1]
        cols = slice(pair * 2 * dim, (pair + 1) * 2 * dim)
        o_ref[:half, cols] = jnp.concatenate([one[:, :dim], two[:, :dim]], axis=-1)
        o_ref[half:, cols] = jnp.concatenate([one[:, dim:], two[:, dim:]], axis=-1)


def padded_queries(packed, dim):
    wide = packed.astype(jnp.float32)
    low = lanes_of(wide.shape) < dim
    top = jnp.where(low, wide, 0.0)
    bottom = jnp.where(low, pltpu.roll(wide, dim, 1), 0.0)
    return jnp.concatenate([top, bottom], axis=0).astype(jnp.bfloat16)


def offset_of(kind, half):
    if kind not in ("near", "far"):
        return kind
    side = 1 - 2 * (lax.axis_index("group") % 2)
    return half + side if kind == "near" else half - side


def dense_bias(lists_ref, counts_ref, offset, block, tile):
    blocks, width = lists_ref.shape[3], lists_ref.shape[1]
    lane = lanes_of((blocks, tile))
    ident = lax.broadcasted_iota(jnp.int32, (blocks, tile), 0)
    found = []
    for first in range(0, blocks, tile // block):
        listed = jnp.zeros((blocks, tile), jnp.int32)
        for n in range(first, first + tile // block):
            here = lane // block == n - first
            number = counts_ref[offset, 0, n]
            for e in range(width):
                entry = jnp.where(e < number, lists_ref[offset, e, 0, n], -1)
                listed = jnp.where(here & (ident == entry), 1, listed)
        found.append(jnp.where(listed > 0, 0.0, -jnp.inf))
    return found


def attend_kernel(dim, dense, kinds, half, first, last, tile, bias_for, *refs):
    refs = list(refs)
    chunk_ref = refs.pop(0)
    sources = [refs.pop(0) for _ in kinds[first:]]
    lists_ref, counts_ref = refs.pop(0), refs.pop(0)
    state_ref = None if first else refs.pop(0)
    out_ref = refs.pop(0)
    query_ref = refs.pop(0) if first else chunk_ref
    blocks = chunk_ref.shape[0]
    block = sources[0].shape[1]
    per = tile // block
    factor = LOG2E / math.sqrt(dim)
    offsets = [offset_of(kind, half) for kind in kinds]
    if first:
        sources = [chunk_ref] + sources
        for n in range(blocks):
            query_ref[n] = padded_queries(chunk_ref[n, block:], dim)

    def values_of(keys):
        return jnp.transpose(keys)[dim:]

    if dense:
        biases = []
        for part, offset in enumerate(offsets):
            if first:
                biases.append(dense_bias(lists_ref, counts_ref, offset, block, tile))
            else:
                biases.append([state_ref[t, dim + 16 :] for t in range(blocks // per)])
        keys = [ref[:, :block].reshape(blocks * block, 2 * dim) for ref in sources]
        values = [values_of(k) for k in keys]
        following = dense_bias(lists_ref, counts_ref, offset_of(bias_for, half), block, tile) if bias_for else None

    def listed(part, n):
        ref, width = sources[part], lists_ref.shape[1]
        at = offsets[part]
        found = jnp.concatenate([ref[lists_ref[at, e, 0, n], :block] for e in range(width)], axis=0)
        place = lax.broadcasted_iota(jnp.int32, (width * block, 1), 0)
        return found, jnp.where(place < counts_ref[at, 0, n] * block, 0.0, -jnp.inf)

    def one_tile(t):
        scores, picked = [], []
        if dense:
            query = query_ref[t * per : (t + 1) * per].reshape(tile, 2 * dim)
            for part in range(len(sources)):
                score = rows_dot(keys[part], query).reshape(blocks, block, tile)
                score = score + biases[part][t][:, None, :]
                scores.append(score.reshape(blocks * block, tile))
        else:
            for part in range(len(sources)):
                both = [listed(part, t * per + i) for i in range(per)]
                picked.append([values_of(k) for k, _ in both])
                scores.append(jnp.concatenate(
                    [rows_dot(k, query_ref[t * per + i]) + bias for i, (k, bias) in enumerate(both)],
                    axis=1,
                ))
        top = functools.reduce(jnp.maximum, [s.max(axis=0, keepdims=True) for s in scores])
        if not first:
            before = state_ref[t, dim : dim + 1]
            top = jnp.maximum(top, before)
        weights = [jnp.exp2((s - top) * factor) for s in scores]
        total = functools.reduce(jnp.add, [w.sum(axis=0, keepdims=True) for w in weights])
        sums = []
        for part, weight in enumerate(weights):
            rounded = weight.astype(jnp.bfloat16)
            if dense:
                sums.append(jnp.dot(values[part], rounded, preferred_element_type=jnp.float32))
            else:
                sums.append(jnp.concatenate([
                    jnp.dot(v, rounded[:, i * block : (i + 1) * block], preferred_element_type=jnp.float32)
                    for i, v in enumerate(picked[part])
                ], axis=1))
        accum = functools.reduce(jnp.add, sums)
        if not first:
            shrink = jnp.exp2((before - top) * factor)
            total = total + state_ref[t, dim + 8 : dim + 9] * shrink
            accum = accum + state_ref[t, :dim] * shrink
        if not last:
            out_ref[t, :dim] = accum
            out_ref[t, dim : dim + 8] = jnp.broadcast_to(top, (8, tile))
            out_ref[t, dim + 8 : dim + 16] = jnp.broadcast_to(total, (8, tile))
            if dense and following is not None:
                out_ref[t, dim + 16 :] = following[t]
            return
        output = accum * (1.0 / total)
        for i in range(0, per, 2):
            pair = output[:, i * block : (i + 2) * block]
            turned = jnp.concatenate([pair, pltpu.roll(pair, 2 * block - block // 2, 1)], axis=0).T
            out_ref[t * per + i] = turned[: block // 2].astype(out_ref.dtype)
            out_ref[t * per + i + 1] = turned[block : block + block // 2].astype(out_ref.dtype)

    if dense:
        for t in range(blocks // per):
            one_tile(t)
    else:
        pl.loop(0, blocks // per)(one_tile)


TILE_BLOCKS = 2


def attend(chunk, kinds, sources, lists, counts, state, last, dense, dim, half, bias_for=None):
    first = state is None
    block = sources[0].shape[1]
    blocks, width = lists.shape[3], lists.shape[1]
    tile = (TILE_BLOCKS if dense else 2) * block
    if last:
        out = jax.ShapeDtypeStruct((blocks, block // 2, 2 * dim), jnp.bfloat16)
    else:
        rows = dim + 16 + (blocks if dense else 0)
        out = jax.ShapeDtypeStruct((blocks * block // tile, rows, tile), jnp.float32)
    outs = (out, jax.ShapeDtypeStruct((blocks, block, 2 * dim), jnp.bfloat16)) if first else (out,)
    vmem = pl.BlockSpec(memory_space=VMEM)
    smem = pl.BlockSpec(memory_space=SMEM)
    args = [chunk, *sources, lists, counts]
    specs = [vmem] * (1 + len(sources)) + [smem, smem]
    if not first:
        args.append(state)
        specs.append(vmem)
    pairs = len(kinds) * blocks * block * (blocks if dense else width) * block
    result = pl.pallas_call(
        functools.partial(attend_kernel, dim, dense, kinds, half, first, last, tile, bias_for),
        out_shape=outs,
        in_specs=specs,
        out_specs=tuple(vmem for _ in outs),
        cost_estimate=pl.CostEstimate(flops=8 * pairs * dim, bytes_accessed=4 * chunk.size, transcendentals=pairs),
        compiler_params=pltpu.CompilerParams(vmem_limit_bytes=VMEM_LIMIT),
        name="attend_last" if last else "attend",
    )(*args)
    return result if first else result[0]


VMEM_LIMIT = 16 << 20


def body(qkv, pattern, counts):
    n_group, n_head = lax.axis_size("group"), lax.axis_size("head")
    half = n_group // 4
    tokens, _, inner = qkv.shape
    dim = inner // n_head
    lists = jnp.transpose(pattern, (1, 3, 0, 2))
    live = jnp.transpose(counts, (1, 0, 2))
    blocks, width = lists.shape[3], lists.shape[1]
    dense = blocks <= 2 * width
    odd = lax.axis_index("group") % 2
    vmem = pl.BlockSpec(memory_space=VMEM)

    packed = pl.pallas_call(
        functools.partial(pack_kernel, dim),
        out_shape=jax.ShapeDtypeStruct((n_head, tokens * 3 // 2, 2 * dim), qkv.dtype),
        compiler_params=pltpu.CompilerParams(vmem_limit_bytes=VMEM_LIMIT),
        name="pack",
    )(jnp.transpose(qkv, (1, 0, 2)))
    chunk = lax.all_to_all(packed, "head", split_axis=0, concat_axis=0, tiled=True)
    own = chunk[:, :tokens]

    def swap(value, shift):
        pairs = []
        for even in range(shift, n_group + shift, 2):
            one, two = even % n_group, (even + 1) % n_group
            pairs += [(one, two), (two, one)]
        return lax.ppermute(value, "group", pairs)

    far = swap(own, 1)
    near = swap(own, 0)
    settings = dict(dense=dense, dim=dim, half=half)
    state, queries = attend(chunk, (half, "near"), [near], lists, live, None, last=False, bias_for="far", **settings)
    state = attend(queries, ("far",), [far], lists, live, state, last=half == 1, **settings)
    ahead = jnp.where(odd == 1, near, far)
    behind = jnp.where(odd == 1, far, near)
    for step in range(2, half + 1):
        ring = [(source, (source + 1) % n_group) for source in range(n_group)]
        ahead = lax.ppermute(ahead, "group", ring)
        behind = lax.ppermute(behind, "group", [(b, a) for a, b in ring])
        for source, offset in ((ahead, half - step), (behind, half + step)):
            last = step == half and offset > half
            state = attend(queries, (offset,), [source], lists, live, state, last=last, **settings)
    returned = lax.all_to_all(state, "head", split_axis=0, concat_axis=0, tiled=True)
    return pl.pallas_call(
        functools.partial(unpack_kernel, dim),
        out_shape=jax.ShapeDtypeStruct((tokens, inner), qkv.dtype),
        in_specs=[vmem],
        compiler_params=pltpu.CompilerParams(vmem_limit_bytes=VMEM_LIMIT),
        name="unpack",
    )(returned)


def solution(mesh):
    return jax.shard_map(
        body,
        mesh=mesh,
        in_specs=(
            P(("group", "head"), None, None),
            P("group", None, None, None),
            P("group", None, None),
        ),
        out_specs=P(("group", "head"), None),
        check_vma=False,
    )
```

```python
import functools
import math

import jax
import jax.numpy as jnp
from jax import lax
from jax.experimental import pallas as pl
from jax.experimental.pallas import tpu as pltpu
from jax.sharding import PartitionSpec as P

LOG2E = 1.4426950408889634
VMEM = pltpu.MemorySpace.VMEM
SMEM = pltpu.MemorySpace.SMEM


def lanes_of(shape):
    return lax.broadcasted_iota(jnp.int32, shape, len(shape) - 1)


def rows_dot(left, right):
    return lax.dot_general(
        left, right, (((1,), (1,)), ((), ())), preferred_element_type=jnp.float32
    )


def pack_kernel(dim, x_ref, o_ref):
    tokens = x_ref.shape[1]
    half = tokens // 2
    for head in range(o_ref.shape[0]):
        cols = slice(head * dim, (head + 1) * dim)
        o_ref[head, :tokens] = jnp.concatenate([x_ref[1, :, cols], x_ref[2, :, cols]], axis=-1)
        o_ref[head, tokens:] = jnp.concatenate(
            [x_ref[0, :half, cols], x_ref[0, half:, cols]], axis=-1
        )


def unpack_kernel(dim, x_ref, o_ref):
    half = x_ref.shape[1]
    for pair in range(x_ref.shape[0] // 2):
        one, two = x_ref[2 * pair], x_ref[2 * pair + 1]
        cols = slice(pair * 2 * dim, (pair + 1) * 2 * dim)
        o_ref[:half, cols] = jnp.concatenate([one[:, :dim], two[:, :dim]], axis=-1)
        o_ref[half:, cols] = jnp.concatenate([one[:, dim:], two[:, dim:]], axis=-1)


def padded_queries(packed, dim):
    wide = packed.astype(jnp.float32)
    low = lanes_of(wide.shape) < dim
    top = jnp.where(low, wide, 0.0)
    bottom = jnp.where(low, pltpu.roll(wide, dim, 1), 0.0)
    return jnp.concatenate([top, bottom], axis=0).astype(jnp.bfloat16)


def offset_of(kind, half):
    if kind not in ("near", "far"):
        return kind
    side = 1 - 2 * (lax.axis_index("group") % 2)
    return half + side if kind == "near" else half - side


def dense_bias(lists_ref, counts_ref, offset, block, tile):
    blocks, width = lists_ref.shape[3], lists_ref.shape[1]
    lane = lanes_of((blocks, tile))
    ident = lax.broadcasted_iota(jnp.int32, (blocks, tile), 0)
    found = []
    for first in range(0, blocks, tile // block):
        listed = jnp.zeros((blocks, tile), jnp.int32)
        for n in range(first, first + tile // block):
            here = lane // block == n - first
            number = counts_ref[offset, 0, n]
            for e in range(width):
                entry = jnp.where(e < number, lists_ref[offset, e, 0, n], -1)
                listed = jnp.where(here & (ident == entry), 1, listed)
        found.append(jnp.where(listed > 0, 0.0, -jnp.inf))
    return found


def attend_kernel(dim, dense, kinds, half, first, last, tile, bias_for, *refs):
    refs = list(refs)
    chunk_ref = refs.pop(0)
    sources = [refs.pop(0) for _ in kinds[first:]]
    if first or not dense:
        lists_ref, counts_ref = refs.pop(0), refs.pop(0)
    state_ref = None if first else refs.pop(0)
    out_ref = refs.pop(0)
    query_ref = refs.pop(0) if first else chunk_ref
    blocks = chunk_ref.shape[0]
    block = sources[0].shape[1]
    per = tile // block
    factor = LOG2E / math.sqrt(dim)
    offsets = [offset_of(kind, half) for kind in kinds]
    if first:
        sources = [chunk_ref] + sources
        for n in range(blocks):
            query_ref[n] = padded_queries(chunk_ref[n, block:], dim)

    def values_of(keys):
        return jnp.transpose(keys)[dim:]

    if dense:
        biases = []
        for part, offset in enumerate(offsets):
            if first:
                biases.append(dense_bias(lists_ref, counts_ref, offset, block, tile))
            else:
                biases.append([state_ref[t, dim + 16 :] for t in range(blocks // per)])
        keys = [ref[:, :block].reshape(blocks * block, 2 * dim) for ref in sources]
        values = [values_of(k) for k in keys]
        following = dense_bias(lists_ref, counts_ref, offset_of(bias_for, half), block, tile) if bias_for else None

    def listed(part, n):
        ref, width = sources[part], lists_ref.shape[1]
        at = offsets[part]
        found = jnp.concatenate([ref[lists_ref[at, e, 0, n], :block] for e in range(width)], axis=0)
        place = lax.broadcasted_iota(jnp.int32, (width * block, 1), 0)
        return found, jnp.where(place < counts_ref[at, 0, n] * block, 0.0, -jnp.inf)

    def one_tile(t):
        scores, picked = [], []
        if dense:
            query = query_ref[t * per : (t + 1) * per].reshape(tile, 2 * dim)
            for part in range(len(sources)):
                score = rows_dot(keys[part], query).reshape(blocks, block, tile)
                score = score + biases[part][t][:, None, :]
                scores.append(score.reshape(blocks * block, tile))
        else:
            for part in range(len(sources)):
                both = [listed(part, t * per + i) for i in range(per)]
                picked.append([values_of(k) for k, _ in both])
                scores.append(jnp.concatenate(
                    [rows_dot(k, query_ref[t * per + i]) + bias for i, (k, bias) in enumerate(both)],
                    axis=1,
                ))
        top = functools.reduce(jnp.maximum, [s.max(axis=0, keepdims=True) for s in scores])
        if not first:
            before = state_ref[t, dim : dim + 1]
            top = jnp.maximum(top, before)
        weights = [jnp.exp2((s - top) * factor) for s in scores]
        total = functools.reduce(jnp.add, [w.sum(axis=0, keepdims=True) for w in weights])
        sums = []
        for part, weight in enumerate(weights):
            rounded = weight.astype(jnp.bfloat16)
            if dense:
                sums.append(jnp.dot(values[part], rounded, preferred_element_type=jnp.float32))
            else:
                sums.append(jnp.concatenate([
                    jnp.dot(v, rounded[:, i * block : (i + 1) * block], preferred_element_type=jnp.float32)
                    for i, v in enumerate(picked[part])
                ], axis=1))
        accum = functools.reduce(jnp.add, sums)
        if not first:
            shrink = jnp.exp2((before - top) * factor)
            total = total + state_ref[t, dim + 8 : dim + 9] * shrink
            accum = accum + state_ref[t, :dim] * shrink
        if not last:
            out_ref[t, :dim] = accum
            out_ref[t, dim : dim + 8] = jnp.broadcast_to(top, (8, tile))
            out_ref[t, dim + 8 : dim + 16] = jnp.broadcast_to(total, (8, tile))
            if dense and following is not None:
                out_ref[t, dim + 16 :] = following[t]
            return
        output = accum * (1.0 / total)
        for i in range(0, per, 2):
            pair = output[:, i * block : (i + 2) * block]
            turned = jnp.concatenate([pair, pltpu.roll(pair, 2 * block - block // 2, 1)], axis=0).T
            out_ref[t * per + i] = turned[: block // 2].astype(out_ref.dtype)
            out_ref[t * per + i + 1] = turned[block : block + block // 2].astype(out_ref.dtype)

    if dense:
        for t in range(blocks // per):
            one_tile(t)
    else:
        pl.loop(0, blocks // per)(one_tile)


TILE_BLOCKS = 8


def attend(chunk, kinds, sources, lists, counts, state, last, dense, dim, half, bias_for=None):
    first = state is None
    block = sources[0].shape[1]
    blocks, width = lists.shape[3], lists.shape[1]
    tile = (TILE_BLOCKS if dense else 2) * block
    if last:
        out = jax.ShapeDtypeStruct((blocks, block // 2, 2 * dim), jnp.bfloat16)
    else:
        rows = dim + 16 + (blocks if dense else 0)
        out = jax.ShapeDtypeStruct((blocks * block // tile, rows, tile), jnp.float32)
    outs = (out, jax.ShapeDtypeStruct((blocks, block, 2 * dim), jnp.bfloat16)) if first else (out,)
    vmem = pl.BlockSpec(memory_space=VMEM)
    smem = pl.BlockSpec(memory_space=SMEM)
    args = [chunk, *sources]
    specs = [vmem] * (1 + len(sources))
    if first or not dense:
        args += [lists, counts]
        specs += [smem, smem]
    if not first:
        args.append(state)
        specs.append(vmem)
    pairs = len(kinds) * blocks * block * (blocks if dense else width) * block
    result = pl.pallas_call(
        functools.partial(attend_kernel, dim, dense, kinds, half, first, last, tile, bias_for),
        out_shape=outs,
        in_specs=specs,
        out_specs=tuple(vmem for _ in outs),
        cost_estimate=pl.CostEstimate(flops=8 * pairs * dim, bytes_accessed=4 * chunk.size, transcendentals=pairs),
        compiler_params=pltpu.CompilerParams(vmem_limit_bytes=VMEM_LIMIT),
        name="attend_last" if last else "attend",
    )(*args)
    return result if first else result[0]


VMEM_LIMIT = 16 << 20


def body(qkv, pattern, counts):
    n_group, n_head = lax.axis_size("group"), lax.axis_size("head")
    half = n_group // 4
    tokens, _, inner = qkv.shape
    dim = inner // n_head
    lists = jnp.transpose(pattern, (1, 3, 0, 2))
    live = jnp.transpose(counts, (1, 0, 2))
    blocks, width = lists.shape[3], lists.shape[1]
    dense = blocks <= 2 * width
    odd = lax.axis_index("group") % 2
    vmem = pl.BlockSpec(memory_space=VMEM)

    packed = pl.pallas_call(
        functools.partial(pack_kernel, dim),
        out_shape=jax.ShapeDtypeStruct((n_head, tokens * 3 // 2, 2 * dim), qkv.dtype),
        compiler_params=pltpu.CompilerParams(vmem_limit_bytes=VMEM_LIMIT),
        name="pack",
    )(jnp.transpose(qkv, (1, 0, 2)))
    chunk = lax.all_to_all(packed, "head", split_axis=0, concat_axis=0, tiled=True)
    own = chunk[:, :tokens]

    def swap(value, shift):
        pairs = []
        for even in range(shift, n_group + shift, 2):
            one, two = even % n_group, (even + 1) % n_group
            pairs += [(one, two), (two, one)]
        return lax.ppermute(value, "group", pairs)

    far = swap(own, 1)
    near = swap(own, 0)
    settings = dict(dense=dense, dim=dim, half=half)
    state, queries = attend(chunk, (half, "near"), [near], lists, live, None, last=False, bias_for="far", **settings)
    state = attend(queries, ("far",), [far], lists, live, state, last=half == 1, **settings)
    ahead = jnp.where(odd == 1, near, far)
    behind = jnp.where(odd == 1, far, near)
    for step in range(2, half + 1):
        ring = [(source, (source + 1) % n_group) for source in range(n_group)]
        ahead = lax.ppermute(ahead, "group", ring)
        behind = lax.ppermute(behind, "group", [(b, a) for a, b in ring])
        for source, offset in ((ahead, half - step), (behind, half + step)):
            last = step == half and offset > half
            state = attend(queries, (offset,), [source], lists, live, state, last=last, **settings)
    returned = lax.all_to_all(state, "head", split_axis=0, concat_axis=0, tiled=True)
    return pl.pallas_call(
        functools.partial(unpack_kernel, dim),
        out_shape=jax.ShapeDtypeStruct((tokens, inner), qkv.dtype),
        in_specs=[vmem],
        compiler_params=pltpu.CompilerParams(vmem_limit_bytes=VMEM_LIMIT),
        name="unpack",
    )(returned)


def solution(mesh):
    return jax.shard_map(
        body,
        mesh=mesh,
        in_specs=(
            P(("group", "head"), None, None),
            P("group", None, None, None),
            P("group", None, None),
        ),
        out_specs=P(("group", "head"), None),
        check_vma=False,
    )
```

```python
import functools
import math

import jax
import jax.numpy as jnp
from jax import lax
from jax.experimental import pallas as pl
from jax.experimental.pallas import tpu as pltpu
from jax.sharding import PartitionSpec as P

LOG2E = 1.4426950408889634
VMEM = pltpu.MemorySpace.VMEM
SMEM = pltpu.MemorySpace.SMEM


def lanes_of(shape):
    return lax.broadcasted_iota(jnp.int32, shape, len(shape) - 1)


def products(left, right):
    return jnp.dot(left, right, preferred_element_type=jnp.float32)


def pack_kernel(dim, x_ref, o_ref):
    tokens = x_ref.shape[1]
    half = tokens // 2
    for head in range(o_ref.shape[0]):
        cols = slice(head * dim, (head + 1) * dim)
        o_ref[head, :tokens] = jnp.concatenate([x_ref[1, :, cols], x_ref[2, :, cols]], axis=-1)
        o_ref[head, tokens:] = jnp.concatenate(
            [x_ref[0, :half, cols], x_ref[0, half:, cols]], axis=-1
        )


def unpack_kernel(dim, x_ref, o_ref):
    half = x_ref.shape[1]
    for pair in range(x_ref.shape[0] // 2):
        one, two = x_ref[2 * pair], x_ref[2 * pair + 1]
        cols = slice(pair * 2 * dim, (pair + 1) * 2 * dim)
        o_ref[:half, cols] = jnp.concatenate([one[:, :dim], two[:, :dim]], axis=-1)
        o_ref[half:, cols] = jnp.concatenate([one[:, dim:], two[:, dim:]], axis=-1)


def padded_queries(packed, dim):
    wide = packed.astype(jnp.float32)
    low = lanes_of(wide.shape) < dim
    top = jnp.where(low, wide, 0.0)
    bottom = jnp.where(low, pltpu.roll(wide, dim, 1), 0.0)
    return jnp.concatenate([top, bottom], axis=0).astype(jnp.bfloat16)


def offset_of(kind, half):
    if kind not in ("near", "far"):
        return kind
    side = 1 - 2 * (lax.axis_index("group") % 2)
    return half + side if kind == "near" else half - side


def dense_bias(lists_ref, counts_ref, offset, block, tile):
    blocks, width = lists_ref.shape[3], lists_ref.shape[1]
    lane = lanes_of((blocks, tile))
    ident = lax.broadcasted_iota(jnp.int32, (blocks, tile), 0)
    found = []
    for first in range(0, blocks, tile // block):
        listed = jnp.zeros((blocks, tile), jnp.int32)
        for n in range(first, first + tile // block):
            here = lane // block == n - first
            number = counts_ref[offset, 0, n]
            for e in range(width):
                entry = jnp.where(e < number, lists_ref[offset, e, 0, n], -1)
                listed = jnp.where(here & (ident == entry), 1, listed)
        found.append(jnp.where(listed > 0, 0.0, -jnp.inf))
    return found


def attend_kernel(dim, dense, kinds, half, first, last, tile, bias_for, *refs):
    refs = list(refs)
    chunk_ref = refs.pop(0)
    sources = [refs.pop(0) for _ in kinds[first:]]
    if first or not dense:
        lists_ref, counts_ref = refs.pop(0), refs.pop(0)
    state_ref = None if first else refs.pop(0)
    out_ref = refs.pop(0)
    query_ref = refs.pop(0) if first else chunk_ref
    blocks, block = sources[0].shape[:2]
    per = tile // block
    factor = LOG2E / math.sqrt(dim)
    offsets = [offset_of(kind, half) for kind in kinds]
    if first:
        sources = [chunk_ref] + sources
        for n in range(blocks):
            at, lanes = divmod(n * block, query_ref.shape[2])
            query_ref[at, :, lanes : lanes + block] = padded_queries(chunk_ref[n, block:], dim).T

    def values_of(keys):
        return jnp.transpose(keys)[dim:]

    if dense:
        biases = []
        for part, offset in enumerate(offsets):
            if first:
                biases.append(dense_bias(lists_ref, counts_ref, offset, block, tile))
            else:
                biases.append([state_ref[t, dim + 16 :] for t in range(blocks // per)])
        keys = [ref[:, :block].reshape(blocks * block, 2 * dim) for ref in sources]
        values = [values_of(k) for k in keys]
        following = dense_bias(lists_ref, counts_ref, offset_of(bias_for, half), block, tile) if bias_for else None

    def listed(part, n):
        ref, width = sources[part], lists_ref.shape[1]
        at = offsets[part]
        found = jnp.concatenate([ref[lists_ref[at, e, 0, n], :block] for e in range(width)], axis=0)
        place = lax.broadcasted_iota(jnp.int32, (width * block, 1), 0)
        return found, jnp.where(place < counts_ref[at, 0, n] * block, 0.0, -jnp.inf)

    def one_tile(t):
        scores, picked = [], []
        if dense:
            query = query_ref[t]
            for part in range(len(sources)):
                score = products(keys[part], query).reshape(blocks, block, tile)
                score = score * factor + biases[part][t][:, None, :]
                scores.append(score.reshape(blocks * block, tile))
        else:
            for part in range(len(sources)):
                both = [listed(part, t * per + i) for i in range(per)]
                picked.append([values_of(k) for k, _ in both])
                scores.append(jnp.concatenate(
                    [products(k, query_ref[t][:, i * block : (i + 1) * block]) * factor + bias for i, (k, bias) in enumerate(both)],
                    axis=1,
                ))
        top = functools.reduce(jnp.maximum, [s.max(axis=0, keepdims=True) for s in scores])
        if not first:
            before = state_ref[t, dim : dim + 1]
            top = jnp.maximum(top, before)
        weights = [jnp.exp2(s - top) for s in scores]
        total = functools.reduce(jnp.add, [w.sum(axis=0, keepdims=True) for w in weights])
        sums = []
        for part, weight in enumerate(weights):
            rounded = weight.astype(jnp.bfloat16)
            if dense:
                sums.append(jnp.dot(values[part], rounded, preferred_element_type=jnp.float32))
            else:
                sums.append(jnp.concatenate([
                    jnp.dot(v, rounded[:, i * block : (i + 1) * block], preferred_element_type=jnp.float32)
                    for i, v in enumerate(picked[part])
                ], axis=1))
        accum = functools.reduce(jnp.add, sums)
        if not first:
            shrink = jnp.exp2(before - top)
            total = total + state_ref[t, dim + 8 : dim + 9] * shrink
            accum = accum + state_ref[t, :dim] * shrink
        if not last:
            out_ref[t, :dim] = accum
            out_ref[t, dim : dim + 8] = jnp.broadcast_to(top, (8, tile))
            out_ref[t, dim + 8 : dim + 16] = jnp.broadcast_to(total, (8, tile))
            if dense and following is not None:
                out_ref[t, dim + 16 :] = following[t]
            return
        output = accum * (1.0 / total)
        low = lanes_of((dim, 2 * block)) % block < block // 2
        for i in range(0, per, 4):
            one = output[:, i * block : (i + 2) * block]
            if per - i < 4:
                merged = [one, pltpu.roll(one, 2 * block - block // 2, 1)]
            else:
                two = output[:, (i + 2) * block : (i + 4) * block]
                merged = [
                    jnp.where(low, one, pltpu.roll(two, block // 2, 1)),
                    jnp.where(low, pltpu.roll(one, 2 * block - block // 2, 1), two),
                ]
            turned = jnp.concatenate(merged, axis=0).astype(out_ref.dtype).T
            for j in range(min(per - i, 4)):
                start = j % 2 * block + j // 2 * (block // 2)
                out_ref[t * per + i + j] = turned[start : start + block // 2]

    if dense:
        for t in range(blocks // per):
            one_tile(t)
    else:
        pl.loop(0, blocks // per)(one_tile)


TILE_BLOCKS = 8


def attend(chunk, kinds, sources, lists, counts, state, last, dense, dim, half, bias_for=None):
    first = state is None
    block = sources[0].shape[1]
    blocks, width = lists.shape[3], lists.shape[1]
    tile = (TILE_BLOCKS if dense else 2) * block
    if last:
        out = jax.ShapeDtypeStruct((blocks, block // 2, 2 * dim), jnp.bfloat16)
    else:
        rows = dim + 16 + (blocks if dense else 0)
        out = jax.ShapeDtypeStruct((blocks * block // tile, rows, tile), jnp.float32)
    outs = (out, jax.ShapeDtypeStruct((blocks * block // tile, 2 * dim, tile), jnp.bfloat16)) if first else (out,)
    vmem = pl.BlockSpec(memory_space=VMEM)
    smem = pl.BlockSpec(memory_space=SMEM)
    args = [chunk, *sources]
    specs = [vmem] * (1 + len(sources))
    if first or not dense:
        args += [lists, counts]
        specs += [smem, smem]
    if not first:
        args.append(state)
        specs.append(vmem)
    pairs = len(kinds) * blocks * block * (blocks if dense else width) * block
    result = pl.pallas_call(
        functools.partial(attend_kernel, dim, dense, kinds, half, first, last, tile, bias_for),
        out_shape=outs,
        in_specs=specs,
        out_specs=tuple(vmem for _ in outs),
        cost_estimate=pl.CostEstimate(flops=8 * pairs * dim, bytes_accessed=4 * chunk.size, transcendentals=pairs),
        compiler_params=pltpu.CompilerParams(
            vmem_limit_bytes=VMEM_LIMIT
        ),
        name="attend_last" if last else "attend",
    )(*args)
    return result if first else result[0]


VMEM_LIMIT = 16 << 20


def body(qkv, pattern, counts):
    n_group, n_head = lax.axis_size("group"), lax.axis_size("head")
    half = n_group // 4
    tokens, _, inner = qkv.shape
    dim = inner // n_head
    lists = jnp.transpose(pattern, (1, 3, 0, 2))
    live = jnp.transpose(counts, (1, 0, 2))
    blocks, width = lists.shape[3], lists.shape[1]
    dense = half == 1 and blocks <= 2 * width
    odd = lax.axis_index("group") % 2
    vmem = pl.BlockSpec(memory_space=VMEM)

    packed = pl.pallas_call(
        functools.partial(pack_kernel, dim),
        out_shape=jax.ShapeDtypeStruct((n_head, tokens * 3 // 2, 2 * dim), qkv.dtype),
        compiler_params=pltpu.CompilerParams(vmem_limit_bytes=VMEM_LIMIT),
        name="pack",
    )(jnp.transpose(qkv, (1, 0, 2)))
    chunk = lax.all_to_all(packed, "head", split_axis=0, concat_axis=0, tiled=True)
    own = chunk[:, :tokens]

    def swap(value, shift):
        pairs = []
        for even in range(shift, n_group + shift, 2):
            one, two = even % n_group, (even + 1) % n_group
            pairs += [(one, two), (two, one)]
        return lax.ppermute(value, "group", pairs)

    far = swap(own, 1)
    near = swap(own, 0)
    settings = dict(dense=dense, dim=dim, half=half)
    state, queries = attend(chunk, (half, "near"), [near], lists, live, None, last=False, bias_for="far", **settings)
    state = attend(queries, ("far",), [far], lists, live, state, last=half == 1, **settings)
    ahead = jnp.where(odd == 1, near, far)
    behind = jnp.where(odd == 1, far, near)
    for step in range(2, half + 1):
        ring = [(source, (source + 1) % n_group) for source in range(n_group)]
        ahead = lax.ppermute(ahead, "group", ring)
        behind = lax.ppermute(behind, "group", [(b, a) for a, b in ring])
        for source, offset in ((ahead, half - step), (behind, half + step)):
            last = step == half and offset > half
            state = attend(queries, (offset,), [source], lists, live, state, last=last, **settings)
    returned = lax.all_to_all(state, "head", split_axis=0, concat_axis=0, tiled=True)
    return pl.pallas_call(
        functools.partial(unpack_kernel, dim),
        out_shape=jax.ShapeDtypeStruct((tokens, inner), qkv.dtype),
        in_specs=[vmem],
        compiler_params=pltpu.CompilerParams(vmem_limit_bytes=VMEM_LIMIT),
        name="unpack",
    )(returned)


def solution(mesh):
    return jax.shard_map(
        body,
        mesh=mesh,
        in_specs=(
            P(("group", "head"), None, None),
            P("group", None, None, None),
            P("group", None, None),
        ),
        out_specs=P(("group", "head"), None),
        check_vma=False,
    )
```

```python
import functools
import math

import jax
import jax.numpy as jnp
from jax import lax
from jax.experimental import pallas as pl
from jax.experimental.pallas import tpu as pltpu
from jax.sharding import PartitionSpec as P

LOG2E = 1.4426950408889634
VMEM = pltpu.MemorySpace.VMEM
SMEM = pltpu.MemorySpace.SMEM


def lanes_of(shape):
    return lax.broadcasted_iota(jnp.int32, shape, len(shape) - 1)


def exchange(value, order):
    return lax.all_to_all(
        value, "head", split_axis=0, concat_axis=0, tiled=True, axis_index_groups=[list(order)]
    )


def products(left, right):
    return jnp.dot(left, right, preferred_element_type=jnp.float32)


def pack_kernel(dim, order, x_ref, o_ref):
    tokens = x_ref.shape[1]
    half = tokens // 2
    for chunk, head in enumerate(order):
        cols = slice(head * dim, (head + 1) * dim)
        o_ref[chunk, :tokens] = jnp.concatenate([x_ref[1, :, cols], x_ref[2, :, cols]], axis=-1)
        o_ref[chunk, tokens:] = jnp.concatenate(
            [x_ref[0, :half, cols], x_ref[0, half:, cols]], axis=-1
        )


def unpack_kernel(dim, order, x_ref, o_ref):
    half = x_ref.shape[1]
    for pair in range(x_ref.shape[0] // 2):
        one, two = x_ref[order.index(2 * pair)], x_ref[order.index(2 * pair + 1)]
        cols = slice(pair * 2 * dim, (pair + 1) * 2 * dim)
        o_ref[:half, cols] = jnp.concatenate([one[:, :dim], two[:, :dim]], axis=-1)
        o_ref[half:, cols] = jnp.concatenate([one[:, dim:], two[:, dim:]], axis=-1)


def padded_queries(packed, dim):
    wide = packed.astype(jnp.float32)
    low = lanes_of(wide.shape) < dim
    top = jnp.where(low, wide, 0.0)
    bottom = jnp.where(low, pltpu.roll(wide, dim, 1), 0.0)
    return jnp.concatenate([top, bottom], axis=0).astype(jnp.bfloat16)


def offset_of(kind, half):
    if kind not in ("near", "far"):
        return kind
    side = 1 - 2 * (lax.axis_index("group") % 2)
    return half + side if kind == "near" else half - side


def dense_bias(lists_ref, counts_ref, offset, block, tile, order):
    blocks, width = lists_ref.shape[3], lists_ref.shape[1]
    lane = lanes_of((blocks, tile))
    place = lax.broadcasted_iota(jnp.int32, (blocks, tile), 0)
    ident = functools.reduce(lambda a, i: jnp.where(place == i, order[i], a), range(blocks), place)
    found = []
    for first in range(0, blocks, tile // block):
        listed = jnp.zeros((blocks, tile), jnp.int32)
        for n in range(first, first + tile // block):
            here = lane // block == n - first
            number = counts_ref[offset, 0, order[n]]
            for e in range(width):
                entry = jnp.where(e < number, lists_ref[offset, e, 0, order[n]], -1)
                listed = jnp.where(here & (ident == entry), 1, listed)
        found.append(jnp.where(listed > 0, 0.0, -jnp.inf))
    return found


def attend_kernel(dim, dense, kinds, half, first, last, tile, bias_for, order, *refs):
    refs = list(refs)
    chunk_ref = refs.pop(0)
    sources = [refs.pop(0) for _ in kinds[first:]]
    if first or not dense:
        lists_ref, counts_ref = refs.pop(0), refs.pop(0)
    state_ref = None if first else refs.pop(0)
    out_ref = refs.pop(0)
    query_ref = refs.pop(0) if first else chunk_ref
    blocks, block = sources[0].shape[:2]
    per = tile // block
    factor = LOG2E / math.sqrt(dim)
    offsets = [offset_of(kind, half) for kind in kinds]
    if first:
        sources = [chunk_ref] + sources
        for n in range(blocks):
            at, lanes = divmod(n * block, query_ref.shape[2])
            query_ref[at, :, lanes : lanes + block] = padded_queries(chunk_ref[n, block:], dim).T

    def values_of(keys):
        return jnp.transpose(keys)[dim:]

    if dense:
        biases = []
        for part, offset in enumerate(offsets):
            if first:
                biases.append(dense_bias(lists_ref, counts_ref, offset, block, tile, order))
            else:
                biases.append([state_ref[t, dim + 16 :] for t in range(blocks // per)])
        keys = [ref[:, :block].reshape(blocks * block, 2 * dim) for ref in sources]
        values = [values_of(k) for k in keys]
        following = dense_bias(lists_ref, counts_ref, offset_of(bias_for, half), block, tile, order) if bias_for else None

    def listed(part, n):
        ref, width = sources[part], lists_ref.shape[1]
        at = offsets[part]
        found = jnp.concatenate([ref[lists_ref[at, e, 0, n], :block] for e in range(width)], axis=0)
        place = lax.broadcasted_iota(jnp.int32, (width * block, 1), 0)
        return found, jnp.where(place < counts_ref[at, 0, n] * block, 0.0, -jnp.inf)

    def one_tile(t):
        scores, picked = [], []
        if dense:
            query = query_ref[t]
            for part in range(len(sources)):
                score = products(keys[part], query).reshape(blocks, block, tile)
                score = score * factor + biases[part][t][:, None, :]
                scores.append(score.reshape(blocks * block, tile))
        else:
            for part in range(len(sources)):
                both = [listed(part, t * per + i) for i in range(per)]
                picked.append([values_of(k) for k, _ in both])
                scores.append(jnp.concatenate(
                    [products(k, query_ref[t][:, i * block : (i + 1) * block]) * factor + bias for i, (k, bias) in enumerate(both)],
                    axis=1,
                ))
        top = functools.reduce(jnp.maximum, [s.max(axis=0, keepdims=True) for s in scores])
        if not first:
            before = state_ref[t, dim : dim + 1]
            top = jnp.maximum(top, before)
        weights = [jnp.exp2(s - top) for s in scores]
        total = functools.reduce(jnp.add, [w.sum(axis=0, keepdims=True) for w in weights])
        sums = []
        for part, weight in enumerate(weights):
            rounded = weight.astype(jnp.bfloat16)
            if dense:
                sums.append(jnp.dot(values[part], rounded, preferred_element_type=jnp.float32))
            else:
                sums.append(jnp.concatenate([
                    jnp.dot(v, rounded[:, i * block : (i + 1) * block], preferred_element_type=jnp.float32)
                    for i, v in enumerate(picked[part])
                ], axis=1))
        accum = functools.reduce(jnp.add, sums)
        if not first:
            shrink = jnp.exp2(before - top)
            total = total + state_ref[t, dim + 8 : dim + 9] * shrink
            accum = accum + state_ref[t, :dim] * shrink
        if not last:
            out_ref[t, :dim] = accum
            out_ref[t, dim : dim + 8] = jnp.broadcast_to(top, (8, tile))
            out_ref[t, dim + 8 : dim + 16] = jnp.broadcast_to(total, (8, tile))
            if dense and following is not None:
                out_ref[t, dim + 16 :] = following[t]
            return
        output = accum * (1.0 / total)
        low = lanes_of((dim, 2 * block)) % block < block // 2
        for i in range(0, per, 4):
            one = output[:, i * block : (i + 2) * block]
            if per - i < 4:
                merged = [one, pltpu.roll(one, 2 * block - block // 2, 1)]
            else:
                two = output[:, (i + 2) * block : (i + 4) * block]
                merged = [
                    jnp.where(low, one, pltpu.roll(two, block // 2, 1)),
                    jnp.where(low, pltpu.roll(one, 2 * block - block // 2, 1), two),
                ]
            turned = jnp.concatenate(merged, axis=0).astype(out_ref.dtype).T
            for j in range(min(per - i, 4)):
                start = j % 2 * block + j // 2 * (block // 2)
                out_ref[t * per + i + j] = turned[start : start + block // 2]

    if dense:
        for t in range(blocks // per):
            one_tile(t)
    else:
        pl.loop(0, blocks // per)(one_tile)


TILE_BLOCKS = 8


def order_of(count):
    middle = min(count // 2 + 1, count - 1)
    return (*range(middle, -1, -1), *range(middle + 1, count))


def attend(chunk, kinds, sources, lists, counts, state, last, dense, dim, half, order, bias_for=None):
    first = state is None
    block = sources[0].shape[1]
    blocks, width = lists.shape[3], lists.shape[1]
    tile = (TILE_BLOCKS if dense else 2) * block
    if last:
        out = jax.ShapeDtypeStruct((blocks, block // 2, 2 * dim), jnp.bfloat16)
    else:
        rows = dim + 16 + (blocks if dense else 0)
        out = jax.ShapeDtypeStruct((blocks * block // tile, rows, tile), jnp.float32)
    outs = (out, jax.ShapeDtypeStruct((blocks * block // tile, 2 * dim, tile), jnp.bfloat16)) if first else (out,)
    vmem = pl.BlockSpec(memory_space=VMEM)
    smem = pl.BlockSpec(memory_space=SMEM)
    args = [chunk, *sources]
    specs = [vmem] * (1 + len(sources))
    if first or not dense:
        args += [lists, counts]
        specs += [smem, smem]
    if not first:
        args.append(state)
        specs.append(vmem)
    pairs = len(kinds) * blocks * block * (blocks if dense else width) * block
    result = pl.pallas_call(
        functools.partial(attend_kernel, dim, dense, kinds, half, first, last, tile, bias_for, order),
        out_shape=outs,
        in_specs=specs,
        out_specs=tuple(vmem for _ in outs),
        cost_estimate=pl.CostEstimate(flops=8 * pairs * dim, bytes_accessed=4 * chunk.size, transcendentals=pairs),
        compiler_params=pltpu.CompilerParams(
            vmem_limit_bytes=VMEM_LIMIT
        ),
        name="attend_last" if last else "attend",
    )(*args)
    return result if first else result[0]


VMEM_LIMIT = 16 << 20


def body(qkv, pattern, counts):
    n_group, n_head = lax.axis_size("group"), lax.axis_size("head")
    half = n_group // 4
    tokens, _, inner = qkv.shape
    dim = inner // n_head
    lists = jnp.transpose(pattern, (1, 3, 0, 2))
    live = jnp.transpose(counts, (1, 0, 2))
    blocks, width = lists.shape[3], lists.shape[1]
    dense = half == 1 and blocks <= 2 * width
    odd = lax.axis_index("group") % 2
    order = order_of(n_head) if dense else tuple(range(n_head))
    vmem = pl.BlockSpec(memory_space=VMEM)

    packed = pl.pallas_call(
        functools.partial(pack_kernel, dim, order),
        out_shape=jax.ShapeDtypeStruct((n_head, tokens * 3 // 2, 2 * dim), qkv.dtype),
        compiler_params=pltpu.CompilerParams(vmem_limit_bytes=VMEM_LIMIT),
        name="pack",
    )(jnp.transpose(qkv, (1, 0, 2)))
    chunk = exchange(packed, order)
    own = chunk[:, :tokens]

    def swap(value, shift):
        pairs = []
        for even in range(shift, n_group + shift, 2):
            one, two = even % n_group, (even + 1) % n_group
            pairs += [(one, two), (two, one)]
        return lax.ppermute(value, "group", pairs)

    far = swap(own, 1)
    near = swap(own, 0)
    settings = dict(dense=dense, dim=dim, half=half, order=order)
    state, queries = attend(chunk, (half, "near"), [near], lists, live, None, last=False, bias_for="far", **settings)
    state = attend(queries, ("far",), [far], lists, live, state, last=half == 1, **settings)
    ahead = jnp.where(odd == 1, near, far)
    behind = jnp.where(odd == 1, far, near)
    for step in range(2, half + 1):
        ring = [(source, (source + 1) % n_group) for source in range(n_group)]
        ahead = lax.ppermute(ahead, "group", ring)
        behind = lax.ppermute(behind, "group", [(b, a) for a, b in ring])
        for source, offset in ((ahead, half - step), (behind, half + step)):
            last = step == half and offset > half
            state = attend(queries, (offset,), [source], lists, live, state, last=last, **settings)
    returned = exchange(state, order)
    return pl.pallas_call(
        functools.partial(unpack_kernel, dim, order),
        out_shape=jax.ShapeDtypeStruct((tokens, inner), qkv.dtype),
        in_specs=[vmem],
        compiler_params=pltpu.CompilerParams(vmem_limit_bytes=VMEM_LIMIT),
        name="unpack",
    )(returned)


def solution(mesh):
    return jax.shard_map(
        body,
        mesh=mesh,
        in_specs=(
            P(("group", "head"), None, None),
            P("group", None, None, None),
            P("group", None, None),
        ),
        out_specs=P(("group", "head"), None),
        check_vma=False,
    )
```

```python
import functools
import math

import jax
import jax.numpy as jnp
from jax import lax
from jax.experimental import pallas as pl
from jax.experimental.pallas import tpu as pltpu
from jax.sharding import PartitionSpec as P

LOG2E = 1.4426950408889634
VMEM = pltpu.MemorySpace.VMEM
SMEM = pltpu.MemorySpace.SMEM


def lanes_of(shape):
    return lax.broadcasted_iota(jnp.int32, shape, len(shape) - 1)


def exchange(value, order):
    return lax.all_to_all(
        value, "head", split_axis=0, concat_axis=0, tiled=True, axis_index_groups=[list(order)]
    )


def products(left, right):
    return jnp.dot(left, right, preferred_element_type=jnp.float32)


def pack_kernel(dim, order, x_ref, o_ref):
    tokens = x_ref.shape[1]
    half = tokens // 2
    for chunk, head in enumerate(order):
        cols = slice(head * dim, (head + 1) * dim)
        o_ref[chunk, :tokens] = jnp.concatenate([x_ref[1, :, cols], x_ref[2, :, cols]], axis=-1)
        o_ref[chunk, tokens:] = jnp.concatenate(
            [x_ref[0, :half, cols], x_ref[0, half:, cols]], axis=-1
        )


def unpack_kernel(dim, order, x_ref, o_ref):
    half = x_ref.shape[1]
    for pair in range(x_ref.shape[0] // 2):
        one, two = x_ref[order.index(2 * pair)], x_ref[order.index(2 * pair + 1)]
        cols = slice(pair * 2 * dim, (pair + 1) * 2 * dim)
        o_ref[:half, cols] = jnp.concatenate([one[:, :dim], two[:, :dim]], axis=-1)
        o_ref[half:, cols] = jnp.concatenate([one[:, dim:], two[:, dim:]], axis=-1)


def padded_queries(packed, dim):
    wide = packed.astype(jnp.float32)
    low = lanes_of(wide.shape) < dim
    top = jnp.where(low, wide, 0.0)
    bottom = jnp.where(low, pltpu.roll(wide, dim, 1), 0.0)
    return jnp.concatenate([top, bottom], axis=0).astype(jnp.bfloat16)


def offset_of(kind, half):
    if kind not in ("near", "far"):
        return kind
    side = 1 - 2 * (lax.axis_index("group") % 2)
    return half + side if kind == "near" else half - side


def dense_bias(lists_ref, counts_ref, offset, block, tile, order):
    blocks, width = lists_ref.shape[3], lists_ref.shape[1]
    lane = lanes_of((blocks, tile))
    place = lax.broadcasted_iota(jnp.int32, (blocks, tile), 0)
    ident = functools.reduce(lambda a, i: jnp.where(place == i, order[i], a), range(blocks), place)
    found = []
    for first in range(0, blocks, tile // block):
        listed = jnp.zeros((blocks, tile), jnp.int32)
        for n in range(first, first + tile // block):
            here = lane // block == n - first
            number = counts_ref[offset, 0, order[n]]
            for e in range(width):
                entry = jnp.where(e < number, lists_ref[offset, e, 0, order[n]], -1)
                listed = jnp.where(here & (ident == entry), 1, listed)
        found.append(jnp.where(listed > 0, 0.0, -jnp.inf))
    return found


def attend_kernel(dim, dense, kinds, half, first, last, tile, bias_for, order, *refs):
    refs = list(refs)
    chunk_ref = refs.pop(0)
    sources = [refs.pop(0) for _ in kinds[first:]]
    if first or not dense:
        lists_ref, counts_ref = refs.pop(0), refs.pop(0)
    state_ref = None if first else refs.pop(0)
    out_ref = refs.pop(0)
    query_ref = refs.pop(0) if first else chunk_ref
    blocks, block = sources[0].shape[:2]
    per = tile // block
    factor = LOG2E / math.sqrt(dim)
    offsets = [offset_of(kind, half) for kind in kinds]
    if first:
        sources = [chunk_ref] + sources
        for n in range(blocks):
            at, lanes = divmod(n * block, query_ref.shape[2])
            query_ref[at, :, lanes : lanes + block] = padded_queries(chunk_ref[n, block:], dim).T

    def values_of(keys):
        return jnp.transpose(keys)[dim:]

    if dense:
        biases = []
        for part, offset in enumerate(offsets):
            if first:
                biases.append(dense_bias(lists_ref, counts_ref, offset, block, tile, order))
            else:
                biases.append([state_ref[t, dim + 16 :] for t in range(blocks // per)])
        keys = [ref[:, :block].reshape(blocks * block, 2 * dim) for ref in sources]
        values = [values_of(k) for k in keys]
        following = dense_bias(lists_ref, counts_ref, offset_of(bias_for, half), block, tile, order) if bias_for else None

    def listed(part, n):
        ref, width = sources[part], lists_ref.shape[1]
        at = offsets[part]
        found = jnp.concatenate([ref[lists_ref[at, e, 0, n], :block] for e in range(width)], axis=0)
        place = lax.broadcasted_iota(jnp.int32, (width * block, 1), 0)
        return found, jnp.where(place < counts_ref[at, 0, n] * block, 0.0, -jnp.inf)

    def one_tile(t):
        scores, picked = [], []
        if dense:
            query = query_ref[t]
            for part in range(len(sources)):
                score = products(keys[part], query).reshape(blocks, block, tile)
                score = score * factor + biases[part][t][:, None, :]
                scores.append(score.reshape(blocks * block, tile))
        else:
            for part in range(len(sources)):
                both = [listed(part, t * per + i) for i in range(per)]
                picked.append([values_of(k) for k, _ in both])
                scores.append(jnp.concatenate(
                    [products(k, query_ref[t][:, i * block : (i + 1) * block]) * factor + bias for i, (k, bias) in enumerate(both)],
                    axis=1,
                ))
        top = functools.reduce(jnp.maximum, [s.max(axis=0, keepdims=True) for s in scores])
        if not first:
            before = state_ref[t, dim : dim + 1]
            top = jnp.maximum(top, before)
        weights = [jnp.exp2(s - top) for s in scores]
        total = functools.reduce(jnp.add, [w.sum(axis=0, keepdims=True) for w in weights])
        sums = []
        for part, weight in enumerate(weights):
            rounded = weight.astype(jnp.bfloat16)
            if dense:
                sums.append(jnp.dot(values[part], rounded, preferred_element_type=jnp.float32))
            else:
                sums.append(jnp.concatenate([
                    jnp.dot(v, rounded[:, i * block : (i + 1) * block], preferred_element_type=jnp.float32)
                    for i, v in enumerate(picked[part])
                ], axis=1))
        accum = functools.reduce(jnp.add, sums)
        if not first:
            shrink = jnp.exp2(before - top)
            total = total + state_ref[t, dim + 8 : dim + 9] * shrink
            accum = accum + state_ref[t, :dim] * shrink
        if not last:
            out_ref[t, :dim] = accum
            out_ref[t, dim : dim + 8] = jnp.broadcast_to(top, (8, tile))
            out_ref[t, dim + 8 : dim + 16] = jnp.broadcast_to(total, (8, tile))
            if dense and following is not None:
                out_ref[t, dim + 16 :] = following[t]
            return
        output = accum * (1.0 / total)
        low = lanes_of((dim, 2 * block)) % block < block // 2
        for i in range(0, per, 4):
            one = output[:, i * block : (i + 2) * block]
            if per - i < 4:
                merged = [one, pltpu.roll(one, 2 * block - block // 2, 1)]
            else:
                two = output[:, (i + 2) * block : (i + 4) * block]
                merged = [
                    jnp.where(low, one, pltpu.roll(two, block // 2, 1)),
                    jnp.where(low, pltpu.roll(one, 2 * block - block // 2, 1), two),
                ]
            turned = jnp.concatenate(merged, axis=0).astype(out_ref.dtype).T
            for j in range(min(per - i, 4)):
                start = j % 2 * block + j // 2 * (block // 2)
                out_ref[t * per + i + j] = turned[start : start + block // 2]

    if dense:
        for t in range(blocks // per):
            one_tile(t)
    else:
        pl.loop(0, blocks // per)(one_tile)


TILE_BLOCKS = 8


EIGHTHS = (5, 1, 3, 2, 0, 6, 7, 4)


def order_of(count):
    if count % 8:
        middle = min(count // 2 + 1, count - 1)
        return (*range(middle, -1, -1), *range(middle + 1, count))
    part = count // 8
    return tuple(eighth * part + i for eighth in EIGHTHS for i in range(part))


def attend(chunk, kinds, sources, lists, counts, state, last, dense, dim, half, order, bias_for=None):
    first = state is None
    block = sources[0].shape[1]
    blocks, width = lists.shape[3], lists.shape[1]
    tile = (TILE_BLOCKS if dense else 2) * block
    if last:
        out = jax.ShapeDtypeStruct((blocks, block // 2, 2 * dim), jnp.bfloat16)
    else:
        rows = dim + 16 + (blocks if dense else 0)
        out = jax.ShapeDtypeStruct((blocks * block // tile, rows, tile), jnp.float32)
    outs = (out, jax.ShapeDtypeStruct((blocks * block // tile, 2 * dim, tile), jnp.bfloat16)) if first else (out,)
    vmem = pl.BlockSpec(memory_space=VMEM)
    smem = pl.BlockSpec(memory_space=SMEM)
    args = [chunk, *sources]
    specs = [vmem] * (1 + len(sources))
    if first or not dense:
        args += [lists, counts]
        specs += [smem, smem]
    if not first:
        args.append(state)
        specs.append(vmem)
    pairs = len(kinds) * blocks * block * (blocks if dense else width) * block
    result = pl.pallas_call(
        functools.partial(attend_kernel, dim, dense, kinds, half, first, last, tile, bias_for, order),
        out_shape=outs,
        in_specs=specs,
        out_specs=tuple(vmem for _ in outs),
        cost_estimate=pl.CostEstimate(flops=8 * pairs * dim, bytes_accessed=4 * chunk.size, transcendentals=pairs),
        compiler_params=pltpu.CompilerParams(
            vmem_limit_bytes=VMEM_LIMIT
        ),
        name="attend_last" if last else "attend",
    )(*args)
    return result if first else result[0]


VMEM_LIMIT = 16 << 20


def body(qkv, pattern, counts):
    n_group, n_head = lax.axis_size("group"), lax.axis_size("head")
    half = n_group // 4
    tokens, _, inner = qkv.shape
    dim = inner // n_head
    lists = jnp.transpose(pattern, (1, 3, 0, 2))
    live = jnp.transpose(counts, (1, 0, 2))
    blocks, width = lists.shape[3], lists.shape[1]
    dense = half == 1 and blocks <= 2 * width
    odd = lax.axis_index("group") % 2
    order = order_of(n_head) if dense else tuple(range(n_head))
    vmem = pl.BlockSpec(memory_space=VMEM)

    packed = pl.pallas_call(
        functools.partial(pack_kernel, dim, order),
        out_shape=jax.ShapeDtypeStruct((n_head, tokens * 3 // 2, 2 * dim), qkv.dtype),
        compiler_params=pltpu.CompilerParams(vmem_limit_bytes=VMEM_LIMIT),
        name="pack",
    )(jnp.transpose(qkv, (1, 0, 2)))
    chunk = exchange(packed, order)
    own = chunk[:, :tokens]

    def swap(value, shift):
        pairs = []
        for even in range(shift, n_group + shift, 2):
            one, two = even % n_group, (even + 1) % n_group
            pairs += [(one, two), (two, one)]
        return lax.ppermute(value, "group", pairs)

    far = swap(own, 1)
    near = swap(own, 0)
    settings = dict(dense=dense, dim=dim, half=half, order=order)
    state, queries = attend(chunk, (half, "near"), [near], lists, live, None, last=False, bias_for="far", **settings)
    state = attend(queries, ("far",), [far], lists, live, state, last=half == 1, **settings)
    ahead = jnp.where(odd == 1, near, far)
    behind = jnp.where(odd == 1, far, near)
    for step in range(2, half + 1):
        ring = [(source, (source + 1) % n_group) for source in range(n_group)]
        ahead = lax.ppermute(ahead, "group", ring)
        behind = lax.ppermute(behind, "group", [(b, a) for a, b in ring])
        for source, offset in ((ahead, half - step), (behind, half + step)):
            last = step == half and offset > half
            state = attend(queries, (offset,), [source], lists, live, state, last=last, **settings)
    returned = exchange(state, order)
    return pl.pallas_call(
        functools.partial(unpack_kernel, dim, order),
        out_shape=jax.ShapeDtypeStruct((tokens, inner), qkv.dtype),
        in_specs=[vmem],
        compiler_params=pltpu.CompilerParams(vmem_limit_bytes=VMEM_LIMIT),
        name="unpack",
    )(returned)


def solution(mesh):
    return jax.shard_map(
        body,
        mesh=mesh,
        in_specs=(
            P(("group", "head"), None, None),
            P("group", None, None, None),
            P("group", None, None),
        ),
        out_specs=P(("group", "head"), None),
        check_vma=False,
    )
```
